32 devices in a mesh: scan: 8 (over z, x), depth: 4 (over y, core).
Axes of the slice: x: 2, y: 2, z: 4, core: 2. Of those that a mesh axis runs over, the one named last changes fastest.
Arguments:
- object_slices: float32 [4, 2, 512, 2048], P('depth', None, 'scan'), may hold values from -1 to 1, as said below
- probe_wave: float32 [2, 128, 128], replicated, may hold values from -4 to 4
- offsets: int32 [128, 2], P('scan'), may hold values from 0 to 1920, as said below
- intensity: float32 [128, 128, 128], P('scan'), may hold values from 0 to 1
Outputs:
- gradient: float32 [4, 2, 512, 2048], P('depth', None, 'scan')
The draws below stay inside these ranges and needn't reach their ends.
Inputs may be any that keep to these rules, and one draw needn't show every extreme that they name: `offsets`: position k has its row offset between max(0, (k // 16) * 64 - 64) and min(384, (k // 16) * 64 + 2 * 64 - 128), both ends reached on every scan device, and its column offset between 0 and 1920, both reached on every scan device. `object_slices`: each entry has magnitude at most 1.
All inputs are finite; a program needn't handle non-finite values.
Results may differ from the reference program's by a relative error of at most 0.007.
Values may be sent and summed in bfloat16 or wider, within the bound.
A program may use at most 64 MiB of HBM per device.

```python
import math
import jax
import jax.numpy as jnp
from jax import lax

WAVE = 128
STRIP = 64
NX = 2048
POS_DEV = 16
SLICES = 4
NY = 512
POS = 128


def draw_object_slices(key, part):
    amplitude_key, phase_key = jax.random.split(jax.random.fold_in(key, 11))
    amplitude = jax.random.uniform(amplitude_key, (SLICES, NY, NX), jnp.float32, 0.93, 1.0)
    phase_values = jax.random.uniform(phase_key, (SLICES, NY, NX), jnp.float32, -math.pi, math.pi)
    return jnp.stack([amplitude * jnp.cos(phase_values), amplitude * jnp.sin(phase_values)], axis=1)


def draw_offsets(key, part):
    row_key, col_key = jax.random.split(jax.random.fold_in(key, 23))
    position_index = jnp.arange(POS, dtype=jnp.int32)
    owner_index = position_index // POS_DEV
    row_low = jnp.maximum(0, owner_index * STRIP - STRIP)
    row_high = jnp.minimum(NY - WAVE, owner_index * STRIP + 2 * STRIP - WAVE)
    row_starts = row_low + jax.random.randint(row_key, (POS,), 0, row_high - row_low + 1)
    rank_in_device = position_index % POS_DEV
    row_starts = jnp.where(rank_in_device == 0, row_high, jnp.where(rank_in_device == 1, row_low, row_starts))
    col_starts = jax.random.randint(col_key, (POS,), 0, NX - WAVE + 1)
    col_starts = jnp.where(rank_in_device == 0, NX - WAVE, jnp.where(rank_in_device == 1, 0, col_starts))
    return jnp.stack([row_starts, col_starts], axis=1).astype(jnp.int32)


def steps_of(rng, dims, pieces, low, largest):
    loudness = 1.0
    for axis_at, blocks in pieces:
        heights = jax.random.uniform(jax.random.fold_in(jax.random.fold_in(rng, 6), axis_at), (blocks,), jnp.float32, low / len(pieces), largest / len(pieces))
        loudness = loudness * jnp.repeat(jnp.exp(heights), dims[axis_at] // blocks).reshape((-1,) + (1,) * (len(dims) - 1 - axis_at))
    return loudness


def gaussian(stream_key, dims, deviation, limit, held_as=jnp.bfloat16):
    entries = deviation * jax.random.normal(stream_key, dims, jnp.float32)
    return jnp.clip(entries, min=-limit, max=limit).astype(held_as)


def setup_inputs(seed: int = 0) -> dict:
    key_list = jax.random.split(jax.random.key(seed), 5)
    return {
        "object_slices": draw_object_slices(jax.random.fold_in(key_list[4], 71), 0),
        "probe_wave": gaussian(key_list[1], (2, WAVE, WAVE), 0.7, 4.0, jnp.float32),
        "offsets": draw_offsets(jax.random.fold_in(key_list[4], 71), 0),
        "intensity": jnp.clip(1.0 * jax.random.uniform(key_list[3], (POS, WAVE, WAVE), jnp.float32) ** steps_of(key_list[3], (POS, WAVE, WAVE), ((0, 8),), -0.2, 0.2), 0.0, 1.0),
    }


FRESNEL = 0.0024
HIGHEST = lax.Precision.HIGHEST

def transform_tables(extent):
    position_index = jnp.arange(extent, dtype=jnp.int32)
    product = position_index[:, None] * position_index[None, :] % extent
    phases = -2.0 * math.pi / extent * product.astype(jnp.float32)
    scaling = 1.0 / math.sqrt(extent)
    return (jnp.cos(phases) * scaling, jnp.sin(phases) * scaling)

def kernel_table(extent):
    position_index = jnp.arange(extent, dtype=jnp.int32)
    signed = jnp.where(position_index < extent // 2, position_index, position_index - extent).astype(jnp.float32)
    square = signed * signed
    phases = -math.pi * FRESNEL * (square[:, None] + square[None, :])
    return jnp.stack([jnp.cos(phases), jnp.sin(phases)], axis=0)[None]

def left_product(matrix, field_in):
    real_part, imag_part = (field_in[:, 0], field_in[:, 1])
    out_real = jnp.einsum('jk,bkl->bjl', matrix[0], real_part, precision=HIGHEST) - jnp.einsum('jk,bkl->bjl', matrix[1], imag_part, precision=HIGHEST)
    out_imag = jnp.einsum('jk,bkl->bjl', matrix[0], imag_part, precision=HIGHEST) + jnp.einsum('jk,bkl->bjl', matrix[1], real_part, precision=HIGHEST)
    return jnp.stack([out_real, out_imag], axis=1)

def right_product(field_in, matrix):
    real_part, imag_part = (field_in[:, 0], field_in[:, 1])
    out_real = jnp.einsum('bjk,kl->bjl', real_part, matrix[0], precision=HIGHEST) - jnp.einsum('bjk,kl->bjl', imag_part, matrix[1], precision=HIGHEST)
    out_imag = jnp.einsum('bjk,kl->bjl', imag_part, matrix[0], precision=HIGHEST) + jnp.einsum('bjk,kl->bjl', real_part, matrix[1], precision=HIGHEST)
    return jnp.stack([out_real, out_imag], axis=1)

def spectrum(field_in, matrix):
    return right_product(left_product(matrix, field_in), matrix)

def complex_times(first, second):
    out_real = first[:, 0] * second[:, 0] - first[:, 1] * second[:, 1]
    out_imag = first[:, 0] * second[:, 1] + first[:, 1] * second[:, 0]
    return jnp.stack([out_real, out_imag], axis=1)

def conjugate(field_in):
    return jnp.stack([field_in[:, 0], -field_in[:, 1]], axis=1)

def propagate(field_in, forward, backward, kernel):
    return spectrum(complex_times(spectrum(field_in, forward), kernel), backward)

def retreat(field_in, forward, backward, kernel):
    return spectrum(complex_times(spectrum(field_in, backward), conjugate(kernel)), forward)

def reference(object_slices, probe_wave, offsets, intensity):
    extent = probe_wave.shape[-1]
    forward = transform_tables(extent)
    backward = (forward[0], -forward[1])
    kernel = kernel_table(extent)
    positions = offsets.shape[0]
    window_span = jnp.arange(extent, dtype=jnp.int32)
    row_index = offsets[:, 0][:, None, None] + window_span[None, :, None]
    col_index = offsets[:, 1][:, None, None] + window_span[None, None, :]

    def cut_patches(layer_in):
        return jnp.moveaxis(layer_in[:, row_index, col_index], 0, 1)
    wave_in = jnp.broadcast_to(probe_wave, (positions,) + probe_wave.shape).astype(jnp.float32)
    entered = []
    excited = wave_in
    for slice_index in range(SLICES):
        entered.append(wave_in)
        excited = complex_times(cut_patches(object_slices[slice_index]), wave_in)
        if slice_index < SLICES - 1:
            propagated = propagate(excited, forward, backward, kernel).astype(jnp.bfloat16)
            wave_in = lax.optimization_barrier(propagated).astype(jnp.float32)
    far_field = spectrum(excited, forward)
    misfit = far_field[:, 0] * far_field[:, 0] + far_field[:, 1] * far_field[:, 1] - intensity
    adjoint = spectrum(far_field * misfit[:, None], backward)
    gradients = [None] * SLICES
    for slice_index in range(SLICES - 1, -1, -1):
        contribution = complex_times(conjugate(entered[slice_index]), adjoint)
        empty = jnp.zeros(object_slices.shape[1:], jnp.float32)
        gradients[slice_index] = empty.at[:, row_index, col_index].add(jnp.moveaxis(contribution, 1, 0))
        if slice_index > 0:
            masked = complex_times(conjugate(cut_patches(object_slices[slice_index])), adjoint)
            propagated = retreat(masked, forward, backward, kernel).astype(jnp.bfloat16)
            adjoint = lax.optimization_barrier(propagated).astype(jnp.float32)
    return jnp.stack(gradients, axis=0)
```

```python
import functools
import math

import jax
import jax.numpy as jnp
import numpy as np
from jax import lax
from jax.experimental import pallas as pl
from jax.experimental.pallas import tpu as pltpu
from jax.sharding import PartitionSpec as P

FRESNEL = 0.0024
MESH = pl.DeviceIdType.MESH
HOP_LAG = 3
HALO_TYPE = jnp.float16


def block_tables(extent):
    index = np.arange(extent)
    phases = -2.0 * math.pi / extent * (index[:, None] * index[None, :] % extent)
    real, imag = (np.cos(phases) / math.sqrt(extent), np.sin(phases) / math.sqrt(extent))
    direct = np.block([[real, imag], [-imag, real]]).astype(np.float32)
    conjugated = np.block([[real, -imag], [imag, real]]).astype(np.float32)
    tables = []
    for matrix in (direct, conjugated):
        high = matrix.astype(jnp.bfloat16)
        tables += [high, (matrix - high.astype(np.float32)).astype(jnp.bfloat16)]
    return np.stack(tables)


def kernel_table(extent):
    index = np.arange(extent)
    signed = np.where(index < extent // 2, index, index - extent).astype(np.float64)
    square = signed * signed
    phases = -math.pi * FRESNEL * (square[:, None] + square[None, :])
    return np.stack([np.cos(phases), np.sin(phases)]).astype(np.float32)


def times(first, second):
    return (
        first[0] * second[0] - first[1] * second[1],
        first[0] * second[1] + first[1] * second[0],
    )


def conj_times(first, second):
    return (
        first[0] * second[0] + first[1] * second[1],
        first[0] * second[1] - first[1] * second[0],
    )


def split(value):
    high = value.astype(jnp.bfloat16)
    return high, (value - high.astype(jnp.float32)).astype(jnp.bfloat16)


def dot(first, second):
    return jnp.dot(first, second, preferred_element_type=jnp.float32)


def right_product(field, high, low):
    extent = field[0].shape[1]
    value_high, value_low = split(jnp.concatenate(field, axis=1))
    out = dot(value_high, high) + dot(value_low, high) + dot(value_high, low)
    return out[:, :extent], out[:, extent:]


def left_product(high, low, field):
    extent = field[0].shape[0]
    width = field[0].shape[1]
    value_high, value_low = split(jnp.concatenate(field, axis=0))
    both = dot(high, jnp.concatenate([value_high, value_low], axis=1))
    out = both[:, :width] + both[:, width:] + dot(low, value_high)
    return out[:extent], out[extent:]


def aligned_place(offset, unit, length, taken):
    start = jnp.minimum(offset // unit * unit, length - taken)
    return pl.multiple_of(start, unit), offset - start


def pipeline_kernel(
    sections,
    patches,
    probe_ref,
    intensity_ref,
    tables_ref,
    kernel_ref,
    out_ref,
    psi_in,
    psi_out,
    chi_in,
    chi_out,
    wave,
    own,
    adjoint,
    psi_send,
    psi_recv,
    chi_send,
    chi_recv,
):
    section = lax.axis_index("depth")
    final = sections - 1
    positions, extent = (out_ref.shape[0], out_ref.shape[-1])
    following = lax.rem(section + 1, sections)
    previous = lax.rem(section + sections - 1, sections)

    barrier = pltpu.get_barrier_semaphore()
    for neighbour in (previous, following):
        pl.semaphore_signal(barrier, inc=1, device_id={"depth": neighbour}, device_id_type=MESH)
    pl.semaphore_wait(barrier, 2)

    def psi_copy(index):
        return pltpu.make_async_remote_copy(
            src_ref=psi_out.at[index],
            dst_ref=psi_in.at[index],
            send_sem=psi_send.at[index],
            recv_sem=psi_recv.at[index],
            device_id={"depth": following},
            device_id_type=MESH,
        )

    def chi_copy(index):
        return pltpu.make_async_remote_copy(
            src_ref=chi_out.at[index],
            dst_ref=chi_in.at[index],
            send_sem=chi_send.at[index],
            recv_sem=chi_recv.at[index],
            device_id={"depth": previous},
            device_id_type=MESH,
        )

    def direct():
        return tables_ref[0], tables_ref[1]

    def conjugated():
        return tables_ref[2], tables_ref[3]

    def forward_load(index):
        @pl.when(section == 0)
        def _():
            wave[index] = probe_ref[...]

        @pl.when(section > 0)
        def _():
            psi_copy(index).wait_recv()
            wave[index] = psi_in[index].astype(jnp.float32)

    def forward_compute(index):
        patch = (patches[index, 0], patches[index, 1])
        excited = times(patch, (wave[index, 0], wave[index, 1]))
        far = left_product(*conjugated(), right_product(excited, *direct()))
        misfit = far[0] * far[0] + far[1] * far[1] - intensity_ref[index]
        is_last = section == final
        multiplier = (
            jnp.where(is_last, misfit, kernel_ref[0]),
            jnp.where(is_last, 0.0, kernel_ref[1]),
        )
        result = left_product(
            *direct(), right_product(times(multiplier, far), *conjugated())
        )
        for part in range(2):
            own[lax.rem(index, 2), part] = result[part]
            psi_out[index, part] = result[part].astype(jnp.bfloat16)

    def forward_send(index):
        @pl.when(section < final)
        def _():
            psi_copy(index).start()

    def backward_load(index):
        @pl.when(section == final)
        def _():
            adjoint[...] = own[lax.rem(index, 2)]

        @pl.when(section < final)
        def _():
            chi_copy(index).wait_recv()
            adjoint[...] = chi_in[index].astype(jnp.float32)

    def backward_gradient(index):
        chi = (adjoint[0], adjoint[1])
        term = conj_times((wave[index, 0], wave[index, 1]), chi)
        for part in range(2):
            out_ref[index, part] = term[part]

    def backward_compute(index):
        chi = (adjoint[0], adjoint[1])
        masked = conj_times((patches[index, 0], patches[index, 1]), chi)
        far = left_product(*direct(), right_product(masked, *conjugated()))
        kernel = (kernel_ref[0], kernel_ref[1])
        result = left_product(
            *conjugated(), right_product(conj_times(kernel, far), *direct())
        )
        for part in range(2):
            chi_out[index, part] = result[part].astype(jnp.bfloat16)

    def backward_send(index):
        @pl.when(section > 0)
        def _():
            chi_copy(index).start()

    lag = jnp.minimum(HOP_LAG * (final - section) + 1, positions)

    def forward_only(step, carry):
        forward_load(step)
        forward_compute(step)
        forward_send(step)
        return carry

    def both(step, carry):
        index = step - lag
        forward_load(step)
        backward_load(index)
        forward_compute(step)
        backward_gradient(index)
        backward_compute(index)
        forward_send(step)
        backward_send(index)
        return carry

    def backward_only(step, carry):
        index = step - lag
        backward_load(index)
        backward_gradient(index)

        @pl.when(section > 0)
        def _():
            backward_compute(index)

        backward_send(index)
        return carry

    lax.fori_loop(0, lag, forward_only, 0)
    lax.fori_loop(lag, positions, both, 0)
    lax.fori_loop(positions, positions + lag, backward_only, 0)

    def drain(index, carry):
        @pl.when(section < final)
        def _():
            psi_copy(index).wait_send()

        @pl.when(section > 0)
        def _():
            chi_copy(index).wait_send()

        return carry

    lax.fori_loop(0, positions, drain, 0)


def pipeline(sections, patches, probe, intensity):
    positions, extent = (intensity.shape[0], intensity.shape[-1])
    vmem = pl.BlockSpec(memory_space=pltpu.VMEM)
    waves = (positions, 2, extent, extent)
    semaphores = pltpu.SemaphoreType.DMA((positions,))
    return pl.pallas_call(
        functools.partial(pipeline_kernel, sections),
        out_shape=jax.ShapeDtypeStruct(waves, jnp.float32),
        in_specs=[vmem] * 5,
        out_specs=vmem,
        scratch_shapes=[
            pltpu.VMEM(waves, jnp.bfloat16),
            pltpu.VMEM(waves, jnp.bfloat16),
            pltpu.VMEM(waves, jnp.bfloat16),
            pltpu.VMEM(waves, jnp.bfloat16),
            pltpu.VMEM(waves, jnp.float32),
            pltpu.VMEM((2, 2, extent, extent), jnp.float32),
            pltpu.VMEM((2, extent, extent), jnp.float32),
            semaphores,
            semaphores,
            semaphores,
            semaphores,
        ],
        compiler_params=pltpu.CompilerParams(
            collective_id=0, has_side_effects=True, vmem_limit_bytes=48 * 1024 * 1024
        ),
    )(
        patches,
        probe,
        intensity,
        jnp.asarray(block_tables(extent)),
        jnp.asarray(kernel_table(extent)),
    )


def cut_kernel(rows_ref, cols_ref, layer_ref, out_ref):
    positions, extent = (out_ref.shape[0], out_ref.shape[-1])
    columns = layer_ref.shape[-1]

    def cut_window(index, carry):
        tall, wide = (extent + 8, 2 * extent)
        top, down = aligned_place(rows_ref[index], 8, layer_ref.shape[1], tall)
        start, shift = aligned_place(cols_ref[index], extent, columns, wide)
        for part in range(2):
            block = layer_ref[part, pl.ds(top, tall), pl.ds(start, wide)]
            block = pltpu.roll(block, lax.rem(wide - shift, wide), 1)[:, :extent]
            out_ref[index, part] = pltpu.roll(block, lax.rem(tall - down, tall), 0)[:extent]
        return carry

    lax.fori_loop(0, positions, cut_window, 0)


def cut(row_starts, col_starts, layer, extent):
    smem = pl.BlockSpec(memory_space=pltpu.SMEM)
    vmem = pl.BlockSpec(memory_space=pltpu.VMEM)
    windows = (row_starts.shape[0], 2, extent, extent)
    return pl.pallas_call(
        cut_kernel,
        out_shape=jax.ShapeDtypeStruct(windows, jnp.float32),
        in_specs=[smem, smem, vmem],
        out_specs=vmem,
        compiler_params=pltpu.CompilerParams(vmem_limit_bytes=32 * 1024 * 1024),
    )(row_starts, col_starts, layer)


def scatter_kernel(rows_ref, cols_ref, terms_ref, middle_ref, upper_ref, lower_ref, grid):
    positions, extent = (terms_ref.shape[0], terms_ref.shape[-1])
    columns = grid.shape[-1]
    strip = middle_ref.shape[1]
    grid[...] = jnp.zeros_like(grid)

    def add_window(index, carry):
        tall, wide = (extent + 8, 2 * extent)
        top, down = aligned_place(rows_ref[index], 8, grid.shape[1], tall)
        start, shift = aligned_place(cols_ref[index], extent, columns, wide)
        for part in range(2):
            term = terms_ref[index, part]
            term = jnp.concatenate([term, jnp.zeros((8, extent), term.dtype)], axis=0)
            term = pltpu.roll(term, down, 0)
            term = jnp.concatenate([term, jnp.zeros_like(term)], axis=1)
            place = (part, pl.ds(top, tall), pl.ds(start, wide))
            grid[place] = grid[place] + pltpu.roll(term, shift, 1)
        return carry

    lax.fori_loop(0, positions, add_window, 0)
    upper_ref[...] = grid[:, :strip].astype(upper_ref.dtype)
    middle_ref[...] = grid[:, strip : 2 * strip]
    lower_ref[...] = grid[:, 2 * strip :].astype(lower_ref.dtype)


def scatter(row_starts, col_starts, terms, strip, columns):
    smem = pl.BlockSpec(memory_space=pltpu.SMEM)
    vmem = pl.BlockSpec(memory_space=pltpu.VMEM)
    piece = (2, strip, columns)
    return pl.pallas_call(
        scatter_kernel,
        out_shape=[
            jax.ShapeDtypeStruct(piece, jnp.float32),
            jax.ShapeDtypeStruct(piece, jnp.bfloat16),
            jax.ShapeDtypeStruct(piece, jnp.bfloat16),
        ],
        in_specs=[smem, smem, vmem],
        out_specs=[vmem, vmem, vmem],
        scratch_shapes=[pltpu.VMEM((2, 3 * strip, columns), jnp.float32)],
        compiler_params=pltpu.CompilerParams(vmem_limit_bytes=32 * 1024 * 1024),
    )(row_starts, col_starts, terms)


def shards(scan_peers, sections, object_slices, probe_wave, offsets, intensity):
    layer = object_slices[0]
    strip, columns = layer.shape[1:]
    scan_index = lax.axis_index("scan")
    up = [(i, i + 1) for i in range(scan_peers - 1)]
    down = [(j, i) for i, j in up]
    travelling = layer.astype(HALO_TYPE)
    before = lax.ppermute(travelling, "scan", up)
    after = lax.ppermute(travelling, "scan", down)
    extended = jnp.concatenate(
        [before.astype(jnp.float32), layer, after.astype(jnp.float32)], axis=1
    )
    row_starts = offsets[:, 0] - (scan_index - 1) * strip
    col_starts = offsets[:, 1]
    patches = cut(row_starts, col_starts, extended, probe_wave.shape[-1])
    terms = pipeline(sections, patches, probe_wave, intensity)
    middle, upper, lower = scatter(row_starts, col_starts, terms, strip, columns)
    from_below = lax.ppermute(lower, "scan", up).astype(jnp.float32)
    from_above = lax.ppermute(upper, "scan", down).astype(jnp.float32)
    return (middle + from_below + from_above)[None]


def solution(mesh):
    in_specs = (P("depth", None, "scan", None), P(), P("scan", None), P("scan", None, None))
    out_specs = P("depth", None, "scan", None)
    body = functools.partial(shards, mesh.shape["scan"], mesh.shape["depth"])
    return jax.shard_map(body, mesh=mesh, in_specs=in_specs, out_specs=out_specs, check_vma=False)
```

```python
import functools
import math

import jax
import jax.numpy as jnp
import numpy as np
from jax import lax
from jax.experimental import pallas as pl
from jax.experimental.pallas import tpu as pltpu
from jax.sharding import PartitionSpec as P

FRESNEL = 0.0024
MESH = pl.DeviceIdType.MESH
HOP_LAG = 3
HALO_TYPE = jnp.bfloat16


def block_tables(extent):
    index = np.arange(extent)
    phases = -2.0 * math.pi / extent * (index[:, None] * index[None, :] % extent)
    real, imag = (np.cos(phases) / math.sqrt(extent), np.sin(phases) / math.sqrt(extent))
    direct = np.block([[real, imag], [-imag, real]]).astype(np.float32)
    conjugated = np.block([[real, -imag], [imag, real]]).astype(np.float32)
    tables = []
    for matrix in (direct, conjugated):
        high = matrix.astype(jnp.bfloat16)
        tables += [high, (matrix - high.astype(np.float32)).astype(jnp.bfloat16)]
    return np.stack(tables)


def kernel_table(extent):
    index = np.arange(extent)
    signed = np.where(index < extent // 2, index, index - extent).astype(np.float64)
    square = signed * signed
    phases = -math.pi * FRESNEL * (square[:, None] + square[None, :])
    return np.stack([np.cos(phases), np.sin(phases)]).astype(np.float32)


def times(first, second):
    return (
        first[0] * second[0] - first[1] * second[1],
        first[0] * second[1] + first[1] * second[0],
    )


def conj_times(first, second):
    return (
        first[0] * second[0] + first[1] * second[1],
        first[0] * second[1] - first[1] * second[0],
    )


def split(value):
    high = value.astype(jnp.bfloat16)
    return high, (value - high.astype(jnp.float32)).astype(jnp.bfloat16)


def dot(first, second):
    return jnp.dot(first, second, preferred_element_type=jnp.float32)


def right_product(field, high, low):
    extent = field[0].shape[1]
    value_high, value_low = split(jnp.concatenate(field, axis=1))
    out = dot(value_high, high) + dot(value_low, high) + dot(value_high, low)
    return out[:, :extent], out[:, extent:]


def left_product(high, low, field):
    extent = field[0].shape[0]
    width = field[0].shape[1]
    value_high, value_low = split(jnp.concatenate(field, axis=0))
    both = dot(high, jnp.concatenate([value_high, value_low], axis=1))
    out = both[:, :width] + both[:, width:] + dot(low, value_high)
    return out[:extent], out[extent:]


def aligned_place(offset, unit, length, taken):
    start = jnp.minimum(offset // unit * unit, length - taken)
    return pl.multiple_of(start, unit), offset - start


def pipeline_kernel(
    sections,
    peers,
    own_ref,
    to_next_ref,
    to_prior_ref,
    probe_ref,
    intensity_ref,
    tables_ref,
    kernel_ref,
    out_ref,
    low_in,
    high_in,
    patches,
    top_in,
    bottom_in,
    high_out,
    low_out,
    psi_in,
    psi_out,
    chi_in,
    chi_out,
    wave,
    own,
    adjoint,
    psi_send,
    psi_recv,
    chi_send,
    chi_recv,
    top_send,
    top_recv,
    bottom_send,
    bottom_recv,
    high_send,
    high_recv,
    low_send,
    low_recv,
):
    section = lax.axis_index("depth")
    scan = lax.axis_index("scan")
    final = sections - 1
    has_prior, has_next = (scan > 0, scan < peers - 1)
    positions, extent = (out_ref.shape[0], out_ref.shape[-1])
    half = extent // 2
    following = lax.rem(section + 1, sections)
    previous = lax.rem(section + sections - 1, sections)

    barrier = pltpu.get_barrier_semaphore()
    for neighbour in (previous, following):
        pl.semaphore_signal(barrier, inc=1, device_id={"depth": neighbour}, device_id_type=MESH)
    for exists, peer, empty in (
        (has_prior, scan - 1, (top_in, low_in)),
        (has_next, scan + 1, (bottom_in, high_in)),
    ):

        @pl.when(exists)
        def _():
            pl.semaphore_signal(barrier, inc=1, device_id={"scan": peer}, device_id_type=MESH)

        @pl.when(jnp.logical_not(exists))
        def _():
            for ref in empty:
                ref[...] = jnp.zeros_like(ref)

    greeted = 2 + jnp.where(has_prior, 1, 0) + jnp.where(has_next, 1, 0)
    pl.semaphore_wait(barrier, greeted)

    def scan_copy(source, target, send, recv, step):
        return lambda index: pltpu.make_async_remote_copy(
            src_ref=source.at[index],
            dst_ref=target.at[index],
            send_sem=send.at[index],
            recv_sem=recv.at[index],
            device_id={"scan": scan + step},
            device_id_type=MESH,
        )

    top_copy = scan_copy(to_next_ref, top_in, top_send, top_recv, 1)
    bottom_copy = scan_copy(to_prior_ref, bottom_in, bottom_send, bottom_recv, -1)
    high_copy = scan_copy(high_out, high_in, high_send, high_recv, -1)
    low_copy = scan_copy(low_out, low_in, low_send, low_recv, 1)

    def halo_send(index, carry):
        @pl.when(has_next)
        def _():
            top_copy(index).start()

        @pl.when(has_prior)
        def _():
            bottom_copy(index).start()

        return carry

    lax.fori_loop(0, positions, halo_send, 0)

    def psi_copy(index):
        return pltpu.make_async_remote_copy(
            src_ref=psi_out.at[index],
            dst_ref=psi_in.at[index],
            send_sem=psi_send.at[index],
            recv_sem=psi_recv.at[index],
            device_id={"depth": following},
            device_id_type=MESH,
        )

    def chi_copy(index):
        return pltpu.make_async_remote_copy(
            src_ref=chi_out.at[index],
            dst_ref=chi_in.at[index],
            send_sem=chi_send.at[index],
            recv_sem=chi_recv.at[index],
            device_id={"depth": previous},
            device_id_type=MESH,
        )

    def direct():
        return tables_ref[0], tables_ref[1]

    def conjugated():
        return tables_ref[2], tables_ref[3]

    def forward_load(index):
        @pl.when(has_prior)
        def _():
            top_copy(index).wait_recv()

        @pl.when(has_next)
        def _():
            bottom_copy(index).wait_recv()

        for part in range(2):
            rims = jnp.concatenate([top_in[index, part], bottom_in[index, part]], axis=0)
            patches[index, part] = own_ref[index, part] + rims.astype(jnp.float32)

        @pl.when(section == 0)
        def _():
            wave[index] = probe_ref[...]

        @pl.when(section > 0)
        def _():
            psi_copy(index).wait_recv()
            wave[index] = psi_in[index].astype(jnp.float32)

    def forward_compute(index):
        patch = (patches[index, 0], patches[index, 1])
        excited = times(patch, (wave[index, 0], wave[index, 1]))
        far = left_product(*conjugated(), right_product(excited, *direct()))
        misfit = far[0] * far[0] + far[1] * far[1] - intensity_ref[index]
        is_last = section == final
        multiplier = (
            jnp.where(is_last, misfit, kernel_ref[0]),
            jnp.where(is_last, 0.0, kernel_ref[1]),
        )
        result = left_product(
            *direct(), right_product(times(multiplier, far), *conjugated())
        )
        for part in range(2):
            own[lax.rem(index, 2), part] = result[part]
            psi_out[index, part] = result[part].astype(jnp.bfloat16)

    def forward_send(index):
        @pl.when(section < final)
        def _():
            psi_copy(index).start()

    def backward_load(index):
        @pl.when(section == final)
        def _():
            adjoint[...] = own[lax.rem(index, 2)]

        @pl.when(section < final)
        def _():
            chi_copy(index).wait_recv()
            adjoint[...] = chi_in[index].astype(jnp.float32)

    def backward_gradient(index):
        chi = (adjoint[0], adjoint[1])
        term = conj_times((wave[index, 0], wave[index, 1]), chi)
        for part in range(2):
            out_ref[index, part] = term[part]
            rounded = term[part].astype(jnp.bfloat16)
            high_out[index, part] = rounded[:half]
            low_out[index, part] = rounded[half:]

    def gradient_send(index):
        @pl.when(has_prior)
        def _():
            high_copy(index).start()

        @pl.when(has_next)
        def _():
            low_copy(index).start()

    def backward_compute(index):
        chi = (adjoint[0], adjoint[1])
        masked = conj_times((patches[index, 0], patches[index, 1]), chi)
        far = left_product(*direct(), right_product(masked, *conjugated()))
        kernel = (kernel_ref[0], kernel_ref[1])
        result = left_product(
            *conjugated(), right_product(conj_times(kernel, far), *direct())
        )
        for part in range(2):
            chi_out[index, part] = result[part].astype(jnp.bfloat16)

    def backward_send(index):
        @pl.when(section > 0)
        def _():
            chi_copy(index).start()

    lag = jnp.minimum(HOP_LAG * (final - section) + 1, positions)

    def forward_only(step, carry):
        forward_load(step)
        forward_compute(step)
        forward_send(step)
        return carry

    def both(step, carry):
        index = step - lag
        forward_load(step)
        backward_load(index)
        forward_compute(step)
        backward_gradient(index)
        backward_compute(index)
        forward_send(step)
        backward_send(index)
        gradient_send(index)
        return carry

    def backward_only(step, carry):
        index = step - lag
        backward_load(index)
        backward_gradient(index)

        @pl.when(section > 0)
        def _():
            backward_compute(index)

        backward_send(index)
        gradient_send(index)
        return carry

    lax.fori_loop(0, lag, forward_only, 0)
    lax.fori_loop(lag, positions, both, 0)
    lax.fori_loop(positions, positions + lag, backward_only, 0)

    def drain(index, carry):
        @pl.when(section < final)
        def _():
            psi_copy(index).wait_send()

        @pl.when(section > 0)
        def _():
            chi_copy(index).wait_send()

        @pl.when(has_prior)
        def _():
            bottom_copy(index).wait_send()
            high_copy(index).wait_send()
            low_copy(index).wait_recv()

        @pl.when(has_next)
        def _():
            top_copy(index).wait_send()
            low_copy(index).wait_send()
            high_copy(index).wait_recv()

        return carry

    lax.fori_loop(0, positions, drain, 0)


def pipeline(sections, peers, own, to_next, to_prior, probe, intensity):
    positions, extent = (intensity.shape[0], intensity.shape[-1])
    vmem = pl.BlockSpec(memory_space=pltpu.VMEM)
    waves = (positions, 2, extent, extent)
    halves = (positions, 2, extent // 2, extent)
    semaphores = pltpu.SemaphoreType.DMA((positions,))
    return pl.pallas_call(
        functools.partial(pipeline_kernel, sections, peers),
        out_shape=[
            jax.ShapeDtypeStruct(waves, jnp.float32),
            jax.ShapeDtypeStruct(halves, jnp.bfloat16),
            jax.ShapeDtypeStruct(halves, jnp.bfloat16),
        ],
        in_specs=[vmem] * 7,
        out_specs=[vmem] * 3,
        scratch_shapes=[
            pltpu.VMEM(waves, jnp.float32),
            pltpu.VMEM(halves, HALO_TYPE),
            pltpu.VMEM(halves, HALO_TYPE),
            pltpu.VMEM(halves, jnp.bfloat16),
            pltpu.VMEM(halves, jnp.bfloat16),
            pltpu.VMEM(waves, jnp.bfloat16),
            pltpu.VMEM(waves, jnp.bfloat16),
            pltpu.VMEM(waves, jnp.bfloat16),
            pltpu.VMEM(waves, jnp.bfloat16),
            pltpu.VMEM(waves, jnp.float32),
            pltpu.VMEM((2, 2, extent, extent), jnp.float32),
            pltpu.VMEM((2, extent, extent), jnp.float32),
        ]
        + [semaphores] * 12,
        compiler_params=pltpu.CompilerParams(
            collective_id=0, has_side_effects=True, vmem_limit_bytes=48 * 1024 * 1024
        ),
    )(
        own,
        to_next,
        to_prior,
        probe,
        intensity,
        jnp.asarray(block_tables(extent)),
        jnp.asarray(kernel_table(extent)),
    )


def cut_kernel(
    rows_ref, cols_ref, next_rows, next_cols, prior_rows, prior_cols, layer_ref,
    own_ref, to_next_ref, to_prior_ref, padded,
):
    positions, extent = (own_ref.shape[0], own_ref.shape[-1])
    strip, columns = layer_ref.shape[1:]
    zeros = jnp.zeros((2, strip, columns), jnp.float32)
    padded[:, :strip] = zeros
    padded[:, strip : 2 * strip] = layer_ref[...]
    padded[:, 2 * strip :] = zeros

    def take(out, index, row, column):
        height = out.shape[2]
        tall, wide = (height + 8, 2 * extent)
        top, down = aligned_place(row, 8, padded.shape[1], tall)
        start, shift = aligned_place(column, extent, columns, wide)
        for part in range(2):
            block = padded[part, pl.ds(top, tall), pl.ds(start, wide)]
            block = pltpu.roll(block, lax.rem(wide - shift, wide), 1)[:, :extent]
            block = pltpu.roll(block, lax.rem(tall - down, tall), 0)[:height]
            out[index, part] = block.astype(out.dtype)

    def cut_window(index, carry):
        take(own_ref, index, rows_ref[index], cols_ref[index])
        take(to_next_ref, index, strip + next_rows[index], next_cols[index])
        take(to_prior_ref, index, prior_rows[index], prior_cols[index])
        return carry

    lax.fori_loop(0, positions, cut_window, 0)


def cut(places, layer, extent):
    smem = pl.BlockSpec(memory_space=pltpu.SMEM)
    vmem = pl.BlockSpec(memory_space=pltpu.VMEM)
    positions = places[0].shape[0]
    strip, columns = layer.shape[1:]
    halves = (positions, 2, extent // 2, extent)
    return pl.pallas_call(
        cut_kernel,
        out_shape=[
            jax.ShapeDtypeStruct((positions, 2, extent, extent), jnp.float32),
            jax.ShapeDtypeStruct(halves, HALO_TYPE),
            jax.ShapeDtypeStruct(halves, HALO_TYPE),
        ],
        in_specs=[smem] * 6 + [vmem],
        out_specs=[vmem] * 3,
        scratch_shapes=[pltpu.VMEM((2, 3 * strip, columns), jnp.float32)],
        compiler_params=pltpu.CompilerParams(vmem_limit_bytes=32 * 1024 * 1024),
    )(*places, layer)


def scatter_kernel(
    rows_ref, cols_ref, next_rows, next_cols, prior_rows, prior_cols,
    terms_ref, high_ref, low_ref, out_ref, grid,
):
    positions, extent = (terms_ref.shape[0], terms_ref.shape[-1])
    strip, columns = out_ref.shape[1:]
    grid[...] = jnp.zeros_like(grid)

    def add(source, index, row, column):
        height = source.shape[2]
        tall, wide = (height + 8, 2 * extent)
        top, down = aligned_place(row, 8, grid.shape[1], tall)
        start, shift = aligned_place(column, extent, columns, wide)
        for part in range(2):
            term = source[index, part].astype(jnp.float32)
            term = jnp.concatenate([term, jnp.zeros((8, extent), term.dtype)], axis=0)
            term = pltpu.roll(term, down, 0)
            term = jnp.concatenate([term, jnp.zeros_like(term)], axis=1)
            place = (part, pl.ds(top, tall), pl.ds(start, wide))
            grid[place] = grid[place] + pltpu.roll(term, shift, 1)

    def add_windows(index, carry):
        add(terms_ref, index, rows_ref[index], cols_ref[index])
        add(high_ref, index, strip + next_rows[index], next_cols[index])
        add(low_ref, index, prior_rows[index], prior_cols[index])
        return carry

    lax.fori_loop(0, positions, add_windows, 0)
    out_ref[...] = grid[:, strip : 2 * strip]


def scatter(places, terms, high, low, strip, columns):
    smem = pl.BlockSpec(memory_space=pltpu.SMEM)
    vmem = pl.BlockSpec(memory_space=pltpu.VMEM)
    return pl.pallas_call(
        scatter_kernel,
        out_shape=jax.ShapeDtypeStruct((2, strip, columns), jnp.float32),
        in_specs=[smem] * 6 + [vmem] * 3,
        out_specs=vmem,
        scratch_shapes=[pltpu.VMEM((2, 3 * strip, columns), jnp.float32)],
        compiler_params=pltpu.CompilerParams(vmem_limit_bytes=32 * 1024 * 1024),
    )(*places, terms, high, low)


def shards(peers, sections, object_slices, probe_wave, offsets, intensity):
    layer = object_slices[0]
    strip, columns = layer.shape[1:]
    extent = probe_wave.shape[-1]
    scan_index = lax.axis_index("scan")
    up = [(i, i + 1) for i in range(peers - 1)]
    down = [(j, i) for i, j in up]
    starts = jnp.stack([offsets[:, 0] - (scan_index - 1) * strip, offsets[:, 1]])
    after = lax.ppermute(starts, "scan", down)
    before = lax.ppermute(starts, "scan", up)
    places = [place[i] for place in (starts, after, before) for i in range(2)]
    own, to_next, to_prior = cut(places, layer, extent)
    terms, low, high = pipeline(
        sections, peers, own, to_next, to_prior, probe_wave, intensity
    )
    return scatter(places, terms, high, low, strip, columns)[None]


def solution(mesh):
    in_specs = (P("depth", None, "scan", None), P(), P("scan", None), P("scan", None, None))
    out_specs = P("depth", None, "scan", None)
    body = functools.partial(shards, mesh.shape["scan"], mesh.shape["depth"])
    return jax.shard_map(body, mesh=mesh, in_specs=in_specs, out_specs=out_specs, check_vma=False)
```

```python
import functools
import math

import jax
import jax.numpy as jnp
import numpy as np
from jax import lax
from jax.experimental import pallas as pl
from jax.experimental.pallas import tpu as pltpu
from jax.sharding import PartitionSpec as P

FRESNEL = 0.0024
MESH = pl.DeviceIdType.MESH
HOP_LAG = 6
HALO_TYPE = jnp.bfloat16


def block_tables(extent):
    index = np.arange(extent)
    phases = -2.0 * math.pi / extent * (index[:, None] * index[None, :] % extent)
    real, imag = (np.cos(phases) / math.sqrt(extent), np.sin(phases) / math.sqrt(extent))
    direct = np.block([[real, imag], [-imag, real]]).astype(np.float32)
    conjugated = np.block([[real, -imag], [imag, real]]).astype(np.float32)
    tables = []
    for matrix in (direct, conjugated):
        high = matrix.astype(jnp.bfloat16)
        tables += [high, (matrix - high.astype(np.float32)).astype(jnp.bfloat16)]
    return np.stack(tables)


def kernel_table(extent):
    index = np.arange(extent)
    signed = np.where(index < extent // 2, index, index - extent).astype(np.float64)
    square = signed * signed
    phases = -math.pi * FRESNEL * (square[:, None] + square[None, :])
    return np.stack([np.cos(phases), np.sin(phases)]).astype(np.float32)


def times(first, second):
    return (
        first[0] * second[0] - first[1] * second[1],
        first[0] * second[1] + first[1] * second[0],
    )


def conj_times(first, second):
    return (
        first[0] * second[0] + first[1] * second[1],
        first[0] * second[1] - first[1] * second[0],
    )


def split(value):
    high = value.astype(jnp.bfloat16)
    return high, (value - high.astype(jnp.float32)).astype(jnp.bfloat16)


def dot(first, second):
    return jnp.dot(first, second, preferred_element_type=jnp.float32)


def right_product(field, high, low):
    extent = field[0].shape[1]
    value_high, value_low = split(jnp.concatenate(field, axis=1))
    out = dot(value_high, high) + dot(value_low, high) + dot(value_high, low)
    return out[:, :extent], out[:, extent:]


def left_product(high, low, field):
    extent = field[0].shape[0]
    width = field[0].shape[1]
    value_high, value_low = split(jnp.concatenate(field, axis=0))
    both = dot(high, jnp.concatenate([value_high, value_low], axis=1))
    out = both[:, :width] + both[:, width:] + dot(low, value_high)
    return out[:extent], out[extent:]


def aligned_place(offset, unit, length, taken):
    start = jnp.minimum(offset // unit * unit, length - taken)
    return pl.multiple_of(start, unit), offset - start


def pipeline_kernel(
    sections,
    peers,
    own_ref,
    to_next_ref,
    to_prior_ref,
    probe_ref,
    intensity_ref,
    tables_ref,
    kernel_ref,
    out_ref,
    low_in,
    high_in,
    patches,
    top_in,
    bottom_in,
    high_out,
    low_out,
    psi_in,
    psi_out,
    chi_in,
    chi_out,
    wave,
    own,
    adjoint,
    psi_send,
    psi_recv,
    chi_send,
    chi_recv,
    top_send,
    top_recv,
    bottom_send,
    bottom_recv,
    high_send,
    high_recv,
    low_send,
    low_recv,
):
    section = lax.axis_index("depth")
    scan = lax.axis_index("scan")
    final = sections - 1
    has_prior, has_next = (scan > 0, scan < peers - 1)
    positions, extent = (out_ref.shape[0], out_ref.shape[-1])
    half = extent // 2
    following = lax.rem(section + 1, sections)
    previous = lax.rem(section + sections - 1, sections)

    barrier = pltpu.get_barrier_semaphore()
    for neighbour in (previous, following):
        pl.semaphore_signal(barrier, inc=1, device_id={"depth": neighbour}, device_id_type=MESH)
    for exists, peer, empty in (
        (has_prior, scan - 1, (top_in, low_in)),
        (has_next, scan + 1, (bottom_in, high_in)),
    ):

        @pl.when(exists)
        def _():
            pl.semaphore_signal(barrier, inc=1, device_id={"scan": peer}, device_id_type=MESH)

        @pl.when(jnp.logical_not(exists))
        def _():
            for ref in empty:
                ref[...] = jnp.zeros_like(ref)

    greeted = 2 + jnp.where(has_prior, 1, 0) + jnp.where(has_next, 1, 0)
    pl.semaphore_wait(barrier, greeted)

    def scan_copy(source, target, send, recv, step):
        return lambda index: pltpu.make_async_remote_copy(
            src_ref=source.at[index],
            dst_ref=target.at[index],
            send_sem=send.at[index],
            recv_sem=recv.at[index],
            device_id={"scan": scan + step},
            device_id_type=MESH,
        )

    top_copy = scan_copy(to_next_ref, top_in, top_send, top_recv, 1)
    bottom_copy = scan_copy(to_prior_ref, bottom_in, bottom_send, bottom_recv, -1)
    high_copy = scan_copy(high_out, high_in, high_send, high_recv, -1)
    low_copy = scan_copy(low_out, low_in, low_send, low_recv, 1)

    def halo_send(index, carry):
        @pl.when(has_next)
        def _():
            top_copy(index).start()

        @pl.when(has_prior)
        def _():
            bottom_copy(index).start()

        return carry

    lax.fori_loop(0, positions, halo_send, 0)

    def psi_copy(index):
        return pltpu.make_async_remote_copy(
            src_ref=psi_out.at[index],
            dst_ref=psi_in.at[index],
            send_sem=psi_send.at[index],
            recv_sem=psi_recv.at[index],
            device_id={"depth": following},
            device_id_type=MESH,
        )

    def chi_copy(index):
        return pltpu.make_async_remote_copy(
            src_ref=chi_out.at[index],
            dst_ref=chi_in.at[index],
            send_sem=chi_send.at[index],
            recv_sem=chi_recv.at[index],
            device_id={"depth": previous},
            device_id_type=MESH,
        )

    def direct():
        return tables_ref[0], tables_ref[1]

    def conjugated():
        return tables_ref[2], tables_ref[3]

    def forward_load(index):
        @pl.when(has_prior)
        def _():
            top_copy(index).wait_recv()

        @pl.when(has_next)
        def _():
            bottom_copy(index).wait_recv()

        for part in range(2):
            rims = jnp.concatenate([top_in[index, part], bottom_in[index, part]], axis=0)
            patches[index, part] = own_ref[index, part] + rims.astype(jnp.float32)

        @pl.when(section == 0)
        def _():
            wave[index] = probe_ref[...]

        @pl.when(section > 0)
        def _():
            psi_copy(index).wait_recv()
            wave[index] = psi_in[index].astype(jnp.float32)

    def forward_compute(index):
        patch = (patches[index, 0], patches[index, 1])
        excited = times(patch, (wave[index, 0], wave[index, 1]))
        far = left_product(*conjugated(), right_product(excited, *direct()))
        misfit = far[0] * far[0] + far[1] * far[1] - intensity_ref[index]
        is_last = section == final
        multiplier = (
            jnp.where(is_last, misfit, kernel_ref[0]),
            jnp.where(is_last, 0.0, kernel_ref[1]),
        )
        result = left_product(
            *direct(), right_product(times(multiplier, far), *conjugated())
        )
        for part in range(2):
            own[lax.rem(index, 2), part] = result[part]
            psi_out[index, part] = result[part].astype(jnp.bfloat16)

    def forward_send(index):
        @pl.when(section < final)
        def _():
            psi_copy(index).start()

    def backward_load(index):
        @pl.when(section == final)
        def _():
            adjoint[...] = own[lax.rem(index, 2)]

        @pl.when(section < final)
        def _():
            chi_copy(index).wait_recv()
            adjoint[...] = chi_in[index].astype(jnp.float32)

    def backward_gradient(index):
        chi = (adjoint[0], adjoint[1])
        term = conj_times((wave[index, 0], wave[index, 1]), chi)
        for part in range(2):
            out_ref[index, part] = term[part]
            rounded = term[part].astype(jnp.bfloat16)
            high_out[index, part] = rounded[:half]
            low_out[index, part] = rounded[half:]

    def gradient_send(index):
        @pl.when(has_prior)
        def _():
            high_copy(index).start()

        @pl.when(has_next)
        def _():
            low_copy(index).start()

    def backward_compute(index):
        chi = (adjoint[0], adjoint[1])
        masked = conj_times((patches[index, 0], patches[index, 1]), chi)
        far = left_product(*direct(), right_product(masked, *conjugated()))
        kernel = (kernel_ref[0], kernel_ref[1])
        result = left_product(
            *conjugated(), right_product(conj_times(kernel, far), *direct())
        )
        for part in range(2):
            chi_out[index, part] = result[part].astype(jnp.bfloat16)

    def backward_send(index):
        @pl.when(section > 0)
        def _():
            chi_copy(index).start()

    lag = jnp.minimum(HOP_LAG * (final - section) + 1, positions)

    def forward_only(step, carry):
        forward_load(step)
        forward_compute(step)
        forward_send(step)
        return carry

    def both(step, carry):
        index = step - lag
        forward_load(step)
        backward_load(index)
        forward_compute(step)
        backward_gradient(index)
        backward_compute(index)
        forward_send(step)
        backward_send(index)
        gradient_send(index)
        return carry

    def backward_only(step, carry):
        index = step - lag
        backward_load(index)
        backward_gradient(index)

        @pl.when(section > 0)
        def _():
            backward_compute(index)

        backward_send(index)
        gradient_send(index)
        return carry

    lax.fori_loop(0, lag, forward_only, 0)
    lax.fori_loop(lag, positions, both, 0)
    lax.fori_loop(positions, positions + lag, backward_only, 0)

    def drain(index, carry):
        @pl.when(section < final)
        def _():
            psi_copy(index).wait_send()

        @pl.when(section > 0)
        def _():
            chi_copy(index).wait_send()

        @pl.when(has_prior)
        def _():
            bottom_copy(index).wait_send()
            high_copy(index).wait_send()
            low_copy(index).wait_recv()

        @pl.when(has_next)
        def _():
            top_copy(index).wait_send()
            low_copy(index).wait_send()
            high_copy(index).wait_recv()

        return carry

    lax.fori_loop(0, positions, drain, 0)


def pipeline(sections, peers, own, to_next, to_prior, probe, intensity):
    positions, extent = (intensity.shape[0], intensity.shape[-1])
    vmem = pl.BlockSpec(memory_space=pltpu.VMEM)
    waves = (positions, 2, extent, extent)
    halves = (positions, 2, extent // 2, extent)
    semaphores = pltpu.SemaphoreType.DMA((positions,))
    return pl.pallas_call(
        functools.partial(pipeline_kernel, sections, peers),
        out_shape=[
            jax.ShapeDtypeStruct(waves, jnp.float32),
            jax.ShapeDtypeStruct(halves, jnp.bfloat16),
            jax.ShapeDtypeStruct(halves, jnp.bfloat16),
        ],
        in_specs=[vmem] * 7,
        out_specs=[vmem] * 3,
        scratch_shapes=[
            pltpu.VMEM(waves, jnp.float32),
            pltpu.VMEM(halves, HALO_TYPE),
            pltpu.VMEM(halves, HALO_TYPE),
            pltpu.VMEM(halves, jnp.bfloat16),
            pltpu.VMEM(halves, jnp.bfloat16),
            pltpu.VMEM(waves, jnp.bfloat16),
            pltpu.VMEM(waves, jnp.bfloat16),
            pltpu.VMEM(waves, jnp.bfloat16),
            pltpu.VMEM(waves, jnp.bfloat16),
            pltpu.VMEM(waves, jnp.float32),
            pltpu.VMEM((2, 2, extent, extent), jnp.float32),
            pltpu.VMEM((2, extent, extent), jnp.float32),
        ]
        + [semaphores] * 12,
        compiler_params=pltpu.CompilerParams(
            collective_id=0, has_side_effects=True, vmem_limit_bytes=24 * 1024 * 1024
        ),
    )(
        own,
        to_next,
        to_prior,
        probe,
        intensity,
        jnp.asarray(block_tables(extent)),
        jnp.asarray(kernel_table(extent)),
    )


def cut_kernel(
    rows_ref, cols_ref, next_rows, next_cols, prior_rows, prior_cols, layer_ref,
    own_ref, to_next_ref, to_prior_ref, padded,
):
    positions, extent = (own_ref.shape[0], own_ref.shape[-1])
    strip, columns = layer_ref.shape[1:]
    zeros = jnp.zeros((2, strip, columns), jnp.float32)
    padded[:, :strip] = zeros
    padded[:, strip : 2 * strip] = layer_ref[...]
    padded[:, 2 * strip :] = zeros

    def take(out, index, row, column):
        height = out.shape[2]
        tall, wide = (height + 8, 2 * extent)
        top, down = aligned_place(row, 8, padded.shape[1], tall)
        start, shift = aligned_place(column, extent, columns, wide)
        for part in range(2):
            block = padded[part, pl.ds(top, tall), pl.ds(start, wide)]
            block = pltpu.roll(block, lax.rem(wide - shift, wide), 1)[:, :extent]
            block = pltpu.roll(block, lax.rem(tall - down, tall), 0)[:height]
            out[index, part] = block.astype(out.dtype)

    def cut_window(index, carry):
        take(own_ref, index, rows_ref[index], cols_ref[index])
        take(to_next_ref, index, strip + next_rows[index], next_cols[index])
        take(to_prior_ref, index, prior_rows[index], prior_cols[index])
        return carry

    lax.fori_loop(0, positions, cut_window, 0)


def cut(places, layer, extent):
    smem = pl.BlockSpec(memory_space=pltpu.SMEM)
    vmem = pl.BlockSpec(memory_space=pltpu.VMEM)
    positions = places[0].shape[0]
    strip, columns = layer.shape[1:]
    halves = (positions, 2, extent // 2, extent)
    return pl.pallas_call(
        cut_kernel,
        out_shape=[
            jax.ShapeDtypeStruct((positions, 2, extent, extent), jnp.float32),
            jax.ShapeDtypeStruct(halves, HALO_TYPE),
            jax.ShapeDtypeStruct(halves, HALO_TYPE),
        ],
        in_specs=[smem] * 6 + [vmem],
        out_specs=[vmem] * 3,
        scratch_shapes=[pltpu.VMEM((2, 3 * strip, columns), jnp.float32)],
        compiler_params=pltpu.CompilerParams(vmem_limit_bytes=12 * 1024 * 1024),
    )(*places, layer)


def scatter_kernel(
    rows_ref, cols_ref, next_rows, next_cols, prior_rows, prior_cols,
    terms_ref, high_ref, low_ref, out_ref, grid,
):
    positions, extent = (terms_ref.shape[0], terms_ref.shape[-1])
    strip, columns = out_ref.shape[1:]
    grid[...] = jnp.zeros_like(grid)

    def add(source, index, row, column):
        height = source.shape[2]
        tall, wide = (height + 8, 2 * extent)
        top, down = aligned_place(row, 8, grid.shape[1], tall)
        start, shift = aligned_place(column, extent, columns, wide)
        for part in range(2):
            term = source[index, part].astype(jnp.float32)
            term = jnp.concatenate([term, jnp.zeros((8, extent), term.dtype)], axis=0)
            term = pltpu.roll(term, down, 0)
            term = jnp.concatenate([term, jnp.zeros_like(term)], axis=1)
            place = (part, pl.ds(top, tall), pl.ds(start, wide))
            grid[place] = grid[place] + pltpu.roll(term, shift, 1)

    def add_windows(index, carry):
        add(terms_ref, index, rows_ref[index], cols_ref[index])
        add(high_ref, index, strip + next_rows[index], next_cols[index])
        add(low_ref, index, prior_rows[index], prior_cols[index])
        return carry

    lax.fori_loop(0, positions, add_windows, 0)
    out_ref[...] = grid[:, strip : 2 * strip]


def scatter(places, terms, high, low, strip, columns):
    smem = pl.BlockSpec(memory_space=pltpu.SMEM)
    vmem = pl.BlockSpec(memory_space=pltpu.VMEM)
    return pl.pallas_call(
        scatter_kernel,
        out_shape=jax.ShapeDtypeStruct((2, strip, columns), jnp.float32),
        in_specs=[smem] * 6 + [vmem] * 3,
        out_specs=vmem,
        scratch_shapes=[pltpu.VMEM((2, 3 * strip, columns), jnp.float32)],
        compiler_params=pltpu.CompilerParams(vmem_limit_bytes=12 * 1024 * 1024),
    )(*places, terms, high, low)


def shards(peers, sections, object_slices, probe_wave, offsets, intensity):
    layer = object_slices[0]
    strip, columns = layer.shape[1:]
    extent = probe_wave.shape[-1]
    scan_index = lax.axis_index("scan")
    up = [(i, i + 1) for i in range(peers - 1)]
    down = [(j, i) for i, j in up]
    starts = jnp.stack([offsets[:, 0] - (scan_index - 1) * strip, offsets[:, 1]])
    after = lax.ppermute(starts, "scan", down)
    before = lax.ppermute(starts, "scan", up)
    places = [place[i] for place in (starts, after, before) for i in range(2)]
    own, to_next, to_prior = cut(places, layer, extent)
    terms, low, high = pipeline(
        sections, peers, own, to_next, to_prior, probe_wave, intensity
    )
    return scatter(places, terms, high, low, strip, columns)[None]


def solution(mesh):
    in_specs = (P("depth", None, "scan", None), P(), P("scan", None), P("scan", None, None))
    out_specs = P("depth", None, "scan", None)
    body = functools.partial(shards, mesh.shape["scan"], mesh.shape["depth"])
    return jax.shard_map(body, mesh=mesh, in_specs=in_specs, out_specs=out_specs, check_vma=False)
```

```python
import functools
import math

import jax
import jax.numpy as jnp
import numpy as np
from jax import lax
from jax.experimental import pallas as pl
from jax.experimental.pallas import tpu as pltpu
from jax.sharding import PartitionSpec as P

FRESNEL = 0.0024
MESH = pl.DeviceIdType.MESH
HOP_LAG = 6
AHEAD = 4
BEHIND = 3
HALO_TYPE = jnp.bfloat16


def block_tables(extent):
    index = np.arange(extent)
    phases = -2.0 * math.pi / extent * (index[:, None] * index[None, :] % extent)
    real, imag = (np.cos(phases) / math.sqrt(extent), np.sin(phases) / math.sqrt(extent))
    direct = np.block([[real, imag], [-imag, real]]).astype(np.float32)
    conjugated = np.block([[real, -imag], [imag, real]]).astype(np.float32)
    tables = []
    for matrix in (direct, conjugated):
        high = matrix.astype(jnp.bfloat16)
        tables += [high, (matrix - high.astype(np.float32)).astype(jnp.bfloat16)]
    return np.stack(tables)


def kernel_table(extent):
    index = np.arange(extent)
    signed = np.where(index < extent // 2, index, index - extent).astype(np.float64)
    square = signed * signed
    phases = -math.pi * FRESNEL * (square[:, None] + square[None, :])
    return np.stack([np.cos(phases), np.sin(phases)]).astype(np.float32)


def times(first, second):
    return (
        first[0] * second[0] - first[1] * second[1],
        first[0] * second[1] + first[1] * second[0],
    )


def conj_times(first, second):
    return (
        first[0] * second[0] + first[1] * second[1],
        first[0] * second[1] - first[1] * second[0],
    )


def split(value):
    high = value.astype(jnp.bfloat16)
    return high, (value - high.astype(jnp.float32)).astype(jnp.bfloat16)


def dot(first, second):
    return jnp.dot(first, second, preferred_element_type=jnp.float32)


def right_product(field, high, low):
    extent = field[0].shape[1]
    value_high, value_low = split(jnp.concatenate(field, axis=1))
    out = dot(value_high, high) + dot(value_low, high) + dot(value_high, low)
    return out[:, :extent], out[:, extent:]


def left_product(high, low, field):
    extent = field[0].shape[0]
    width = field[0].shape[1]
    value_high, value_low = split(jnp.concatenate(field, axis=0))
    both = dot(high, jnp.concatenate([value_high, value_low], axis=1))
    out = both[:, :width] + both[:, width:] + dot(low, value_high)
    return out[:extent], out[extent:]


def aligned_place(offset, unit, length, taken):
    start = jnp.minimum(offset // unit * unit, length - taken)
    return pl.multiple_of(start, unit), offset - start


def pipeline_kernel(
    sections,
    peers,
    own_ref,
    mine_ref,
    relay_ref,
    pack_ref,
    unpack_ref,
    probe_ref,
    intensity_ref,
    tables_ref,
    kernel_ref,
    out_ref,
    near_in,
    far_in,
    patches,
    relay_in,
    joined,
    joined_in,
    packed_out,
    psi_in,
    psi_out,
    chi_in,
    chi_out,
    wave,
    own,
    adjoint,
    psi_send,
    psi_recv,
    chi_send,
    chi_recv,
    relay_send,
    relay_recv,
    join_send,
    join_recv,
    pack_send,
    pack_recv,
    onward_send,
    onward_recv,
):
    section = lax.axis_index("depth")
    scan = lax.axis_index("scan")
    final = sections - 1
    even = lax.rem(scan, 2) == 0
    partner = jnp.where(even, scan + 1, scan - 1)
    outward = jnp.where(even, scan - 2, scan + 2)
    inward = jnp.where(even, scan + 2, scan - 2)
    has_outward = (outward >= 0) & (outward < peers)
    has_inward = (inward >= 0) & (inward < peers)
    positions, extent = (out_ref.shape[0], out_ref.shape[-1])
    following = lax.rem(section + 1, sections)
    previous = lax.rem(section + sections - 1, sections)

    barrier = pltpu.get_barrier_semaphore()
    for neighbour in (previous, following):
        pl.semaphore_signal(barrier, inc=1, device_id={"depth": neighbour}, device_id_type=MESH)
    pl.semaphore_signal(barrier, inc=1, device_id={"scan": partner}, device_id_type=MESH)
    for exists, peer, empty in (
        (has_outward, outward, far_in),
        (has_inward, inward, relay_in),
    ):

        @pl.when(exists)
        def _():
            pl.semaphore_signal(barrier, inc=1, device_id={"scan": peer}, device_id_type=MESH)

        @pl.when(jnp.logical_not(exists))
        def _():
            empty[...] = jnp.zeros_like(empty)

    greeted = 3 + jnp.where(has_outward, 1, 0) + jnp.where(has_inward, 1, 0)
    pl.semaphore_wait(barrier, greeted)

    def scan_copy(source, target, send, recv, peer):
        return lambda index: pltpu.make_async_remote_copy(
            src_ref=source.at[index],
            dst_ref=target.at[index],
            send_sem=send.at[index],
            recv_sem=recv.at[index],
            device_id={"scan": peer},
            device_id_type=MESH,
        )

    relay_copy = scan_copy(relay_ref, relay_in, relay_send, relay_recv, outward)
    join_copy = scan_copy(joined, joined_in, join_send, join_recv, partner)
    pack_copy = scan_copy(packed_out, near_in, pack_send, pack_recv, partner)
    onward_copy = scan_copy(near_in, far_in, onward_send, onward_recv, inward)

    def relay_start(index, carry):
        @pl.when(has_outward)
        def _():
            relay_copy(index).start()

        return carry

    def join(index, carry):
        @pl.when(has_inward)
        def _():
            relay_copy(index).wait_recv()

        joined[index] = relay_in[index] + mine_ref[index]
        join_copy(index).start()
        return carry

    def onward(index, carry):
        pack_copy(index).wait_recv()

        @pl.when(has_inward)
        def _():
            onward_copy(index).start()

        return carry

    ahead = min(AHEAD, positions)
    behind = min(BEHIND, positions)
    lax.fori_loop(0, positions, relay_start, 0)
    lax.fori_loop(0, ahead, join, 0)

    def psi_copy(index):
        return pltpu.make_async_remote_copy(
            src_ref=psi_out.at[index],
            dst_ref=psi_in.at[index],
            send_sem=psi_send.at[index],
            recv_sem=psi_recv.at[index],
            device_id={"depth": following},
            device_id_type=MESH,
        )

    def chi_copy(index):
        return pltpu.make_async_remote_copy(
            src_ref=chi_out.at[index],
            dst_ref=chi_in.at[index],
            send_sem=chi_send.at[index],
            recv_sem=chi_recv.at[index],
            device_id={"depth": previous},
            device_id_type=MESH,
        )

    def direct():
        return tables_ref[0], tables_ref[1]

    def conjugated():
        return tables_ref[2], tables_ref[3]

    def forward_load(index):
        @pl.when(index + ahead < positions)
        def _():
            join(index + ahead, 0)

        join_copy(index).wait_recv()
        for part in range(2):
            rims = dot(unpack_ref[index], joined_in[index, part])
            patches[index, part] = own_ref[index, part] + rims

        @pl.when(section == 0)
        def _():
            wave[index] = probe_ref[...]

        @pl.when(section > 0)
        def _():
            psi_copy(index).wait_recv()
            wave[index] = psi_in[index].astype(jnp.float32)

    def forward_compute(index):
        patch = (patches[index, 0], patches[index, 1])
        excited = times(patch, (wave[index, 0], wave[index, 1]))
        far = left_product(*conjugated(), right_product(excited, *direct()))
        misfit = far[0] * far[0] + far[1] * far[1] - intensity_ref[index]
        is_last = section == final
        multiplier = (
            jnp.where(is_last, misfit, kernel_ref[0]),
            jnp.where(is_last, 0.0, kernel_ref[1]),
        )
        result = left_product(
            *direct(), right_product(times(multiplier, far), *conjugated())
        )
        for part in range(2):
            own[lax.rem(index, 2), part] = result[part]
            psi_out[index, part] = result[part].astype(jnp.bfloat16)

    def forward_send(index):
        @pl.when(section < final)
        def _():
            psi_copy(index).start()

    def backward_load(index):
        @pl.when(section == final)
        def _():
            adjoint[...] = own[lax.rem(index, 2)]

        @pl.when(section < final)
        def _():
            chi_copy(index).wait_recv()
            adjoint[...] = chi_in[index].astype(jnp.float32)

    def backward_gradient(index):
        chi = (adjoint[0], adjoint[1])
        term = conj_times((wave[index, 0], wave[index, 1]), chi)
        for part in range(2):
            out_ref[index, part] = term[part]
            rims = dot(pack_ref[index], term[part].astype(jnp.bfloat16))
            packed_out[index, part] = rims.astype(jnp.bfloat16)

    def gradient_send(index):
        pack_copy(index).start()

        @pl.when(index >= behind)
        def _():
            onward(index - behind, 0)

    def backward_compute(index):
        chi = (adjoint[0], adjoint[1])
        masked = conj_times((patches[index, 0], patches[index, 1]), chi)
        far = left_product(*direct(), right_product(masked, *conjugated()))
        kernel = (kernel_ref[0], kernel_ref[1])
        result = left_product(
            *conjugated(), right_product(conj_times(kernel, far), *direct())
        )
        for part in range(2):
            chi_out[index, part] = result[part].astype(jnp.bfloat16)

    def backward_send(index):
        @pl.when(section > 0)
        def _():
            chi_copy(index).start()

    lag = jnp.minimum(HOP_LAG * (final - section) + 1, positions)

    def forward_only(step, carry):
        forward_load(step)
        forward_compute(step)
        forward_send(step)
        return carry

    def both(step, carry):
        index = step - lag
        forward_load(step)
        backward_load(index)
        forward_compute(step)
        backward_gradient(index)
        backward_compute(index)
        forward_send(step)
        backward_send(index)
        gradient_send(index)
        return carry

    def backward_only(step, carry):
        index = step - lag
        backward_load(index)
        backward_gradient(index)

        @pl.when(section > 0)
        def _():
            backward_compute(index)

        backward_send(index)
        gradient_send(index)
        return carry

    lax.fori_loop(0, lag, forward_only, 0)
    lax.fori_loop(lag, positions, both, 0)
    lax.fori_loop(positions, positions + lag, backward_only, 0)

    lax.fori_loop(positions - behind, positions, onward, 0)

    def drain(index, carry):
        join_copy(index).wait_send()
        pack_copy(index).wait_send()

        @pl.when(section < final)
        def _():
            psi_copy(index).wait_send()

        @pl.when(section > 0)
        def _():
            chi_copy(index).wait_send()

        @pl.when(has_outward)
        def _():
            relay_copy(index).wait_send()
            onward_copy(index).wait_recv()

        @pl.when(has_inward)
        def _():
            onward_copy(index).wait_send()

        return carry

    lax.fori_loop(0, positions, drain, 0)


def pipeline(sections, peers, pieces, probe, intensity):
    positions, extent = (intensity.shape[0], intensity.shape[-1])
    vmem = pl.BlockSpec(memory_space=pltpu.VMEM)
    waves = (positions, 2, extent, extent)
    halves = (positions, 2, extent // 2, extent)
    semaphores = pltpu.SemaphoreType.DMA((positions,))
    return pl.pallas_call(
        functools.partial(pipeline_kernel, sections, peers),
        out_shape=[
            jax.ShapeDtypeStruct(waves, jnp.float32),
            jax.ShapeDtypeStruct(halves, jnp.bfloat16),
            jax.ShapeDtypeStruct(halves, jnp.bfloat16),
        ],
        in_specs=[vmem] * 9,
        out_specs=[vmem] * 3,
        scratch_shapes=[
            pltpu.VMEM(waves, jnp.float32),
            pltpu.VMEM(halves, HALO_TYPE),
            pltpu.VMEM(halves, HALO_TYPE),
            pltpu.VMEM(halves, jnp.bfloat16),
            pltpu.VMEM(halves, jnp.bfloat16),
            pltpu.VMEM(waves, jnp.bfloat16),
            pltpu.VMEM(waves, jnp.bfloat16),
            pltpu.VMEM(waves, jnp.bfloat16),
            pltpu.VMEM(waves, jnp.bfloat16),
            pltpu.VMEM(waves, jnp.float32),
            pltpu.VMEM((2, 2, extent, extent), jnp.float32),
            pltpu.VMEM((2, extent, extent), jnp.float32),
        ]
        + [semaphores] * 12,
        compiler_params=pltpu.CompilerParams(
            collective_id=0, has_side_effects=True, vmem_limit_bytes=24 * 1024 * 1024
        ),
    )(
        *pieces,
        probe,
        intensity,
        jnp.asarray(block_tables(extent)),
        jnp.asarray(kernel_table(extent)),
    )


def kept_rows(shape, row, above):
    inside = lax.broadcasted_iota(jnp.int32, shape, 0) >= row
    return inside.astype(jnp.int32) == above


def cut_kernel(
    rows_ref, cols_ref, near_rows, near_cols, far_rows, far_cols, even_ref, layer_ref,
    own_ref, mine_ref, relay_ref, pack_ref, unpack_ref, padded,
):
    positions, extent = (own_ref.shape[0], own_ref.shape[-1])
    strip, columns = layer_ref.shape[1:]
    wide = 2 * extent
    zeros = jnp.zeros((2, strip, columns), jnp.float32)
    padded[:, :strip] = zeros
    padded[:, strip : 2 * strip] = layer_ref[...]
    padded[:, 2 * strip :] = zeros

    def take(out, index, row, column, above):
        start, shift = aligned_place(column, extent, columns, wide)
        keep = kept_rows((strip, extent), row, above)
        for part in range(2):
            block = layer_ref[part, :, pl.ds(start, wide)]
            block = pltpu.roll(block, lax.rem(wide - shift, wide), 1)[:, :extent]
            out[index, part] = jnp.where(keep, block, 0.0).astype(out.dtype)

    def cut_window(index, carry):
        tall = extent + 8
        row = rows_ref[index]
        top, down = aligned_place(row, 8, padded.shape[1], tall)
        start, shift = aligned_place(cols_ref[index], extent, columns, wide)
        for part in range(2):
            block = padded[part, pl.ds(top, tall), pl.ds(start, wide)]
            block = pltpu.roll(block, lax.rem(wide - shift, wide), 1)[:, :extent]
            own_ref[index, part] = pltpu.roll(block, lax.rem(tall - down, tall), 0)[:extent]
        even = even_ref[0]
        take(mine_ref, index, near_rows[index], near_cols[index], even)
        take(relay_ref, index, far_rows[index], far_cols[index], 1 - even)
        for ref, strip_axis in ((pack_ref, 0), (unpack_ref, 1)):
            shape = ref.shape[1:]
            strip_row = lax.broadcasted_iota(jnp.int32, shape, strip_axis)
            window_row = lax.broadcasted_iota(jnp.int32, shape, 1 - strip_axis)
            distance = window_row - strip_row + row
            hit = (distance == 0) | (distance == extent)
            ref[index] = jnp.where(hit, 1.0, 0.0).astype(ref.dtype)
        return carry

    lax.fori_loop(0, positions, cut_window, 0)


def cut(places, layer, extent):
    smem = pl.BlockSpec(memory_space=pltpu.SMEM)
    vmem = pl.BlockSpec(memory_space=pltpu.VMEM)
    positions = places[0].shape[0]
    strip, columns = layer.shape[1:]
    halves = (positions, 2, extent // 2, extent)
    return pl.pallas_call(
        cut_kernel,
        out_shape=[
            jax.ShapeDtypeStruct((positions, 2, extent, extent), jnp.float32),
            jax.ShapeDtypeStruct(halves, HALO_TYPE),
            jax.ShapeDtypeStruct(halves, HALO_TYPE),
            jax.ShapeDtypeStruct((positions, extent // 2, extent), jnp.bfloat16),
            jax.ShapeDtypeStruct((positions, extent, extent // 2), jnp.bfloat16),
        ],
        in_specs=[smem] * 7 + [vmem],
        out_specs=[vmem] * 5,
        scratch_shapes=[pltpu.VMEM((2, 3 * strip, columns), jnp.float32)],
        compiler_params=pltpu.CompilerParams(vmem_limit_bytes=12 * 1024 * 1024),
    )(*places, layer)


def scatter_kernel(
    rows_ref, cols_ref, near_rows, near_cols, far_rows, far_cols, even_ref,
    terms_ref, near_ref, far_ref, out_ref, grid,
):
    positions, extent = (terms_ref.shape[0], terms_ref.shape[-1])
    strip, columns = out_ref.shape[1:]
    grid[...] = jnp.zeros_like(grid)

    def add(source, index, row, column):
        height = source.shape[2]
        tall, wide = (height + 8, 2 * extent)
        top, down = aligned_place(row, 8, grid.shape[1], tall)
        start, shift = aligned_place(column, extent, columns, wide)
        for part in range(2):
            term = source[index, part].astype(jnp.float32)
            term = jnp.concatenate([term, jnp.zeros((8, extent), term.dtype)], axis=0)
            term = pltpu.roll(term, down, 0)
            term = jnp.concatenate([term, jnp.zeros_like(term)], axis=1)
            place = (part, pl.ds(top, tall), pl.ds(start, wide))
            grid[place] = grid[place] + pltpu.roll(term, shift, 1)

    def add_rows(source, index, row, column, above):
        wide = 2 * extent
        start, shift = aligned_place(column, extent, columns, wide)
        keep = kept_rows((strip, extent), row, above)
        for part in range(2):
            term = jnp.where(keep, source[index, part].astype(jnp.float32), 0.0)
            term = jnp.concatenate([term, jnp.zeros_like(term)], axis=1)
            place = (part, pl.ds(strip, strip), pl.ds(start, wide))
            grid[place] = grid[place] + pltpu.roll(term, shift, 1)

    def add_windows(index, carry):
        even = even_ref[0]
        add(terms_ref, index, rows_ref[index], cols_ref[index])
        add_rows(near_ref, index, near_rows[index], near_cols[index], even)
        add_rows(far_ref, index, far_rows[index], far_cols[index], 1 - even)
        return carry

    lax.fori_loop(0, positions, add_windows, 0)
    out_ref[...] = grid[:, strip : 2 * strip]


def scatter(places, terms, near, far, strip, columns):
    smem = pl.BlockSpec(memory_space=pltpu.SMEM)
    vmem = pl.BlockSpec(memory_space=pltpu.VMEM)
    return pl.pallas_call(
        scatter_kernel,
        out_shape=jax.ShapeDtypeStruct((2, strip, columns), jnp.float32),
        in_specs=[smem] * 7 + [vmem] * 3,
        out_specs=vmem,
        scratch_shapes=[pltpu.VMEM((2, 3 * strip, columns), jnp.float32)],
        compiler_params=pltpu.CompilerParams(vmem_limit_bytes=12 * 1024 * 1024),
    )(*places, terms, near, far)


def shards(peers, sections, object_slices, probe_wave, offsets, intensity):
    layer = object_slices[0]
    strip, columns = layer.shape[1:]
    extent = probe_wave.shape[-1]
    scan_index = lax.axis_index("scan")
    up = [(i, i + 1) for i in range(peers - 1)]
    down = [(j, i) for i, j in up]
    starts = jnp.stack([offsets[:, 0] - (scan_index - 1) * strip, offsets[:, 1]])
    after = lax.ppermute(starts, "scan", down)
    before = lax.ppermute(starts, "scan", up)
    even = lax.rem(scan_index, 2) == 0
    near = jnp.where(even, after, before)
    far = jnp.where(even, before, after)
    places = [place[i] for place in (starts, near, far) for i in range(2)]
    places.append(jnp.where(even, 1, 0).reshape(1))
    pieces = cut(places, layer, extent)
    terms, near_terms, far_terms = pipeline(sections, peers, pieces, probe_wave, intensity)
    return scatter(places, terms, near_terms, far_terms, strip, columns)[None]


def solution(mesh):
    in_specs = (P("depth", None, "scan", None), P(), P("scan", None), P("scan", None, None))
    out_specs = P("depth", None, "scan", None)
    body = functools.partial(shards, mesh.shape["scan"], mesh.shape["depth"])
    return jax.shard_map(body, mesh=mesh, in_specs=in_specs, out_specs=out_specs, check_vma=False)
```
